32 devices in a mesh: mesh: 8 (over z, core), src: 4 (over y, x).
Axes of the slice: x: 2, y: 2, z: 4, core: 2. Of those that a mesh axis runs over, the one named last changes fastest.
Arguments:
- solution: float32 [512, 24576], P('src', 'mesh'), may hold values from -6 to 6
- conduct: float32 [24576], P('mesh'), may hold values from 0.5 to 2
- source_edge: int32 [512], P('src'), may hold values from 0 to 24575
- source_amp: float32 [512], P('src'), may hold values from -8 to 8
- interior: int32 [8192], P('mesh'), may hold values 0 or 1
- edge_dir: float32 [3, 24576], P(None, 'mesh'), may hold values from -4 to 4
- tail_node: int32 [24576], P('mesh'), may hold values from 0 to 127, as said below
- head_node: int32 [24576], P('mesh'), may hold values from 0 to 383, as said below
- block_inv: float32 [256, 128, 128], P(('mesh', 'src')), may hold values from -1 to 1
- block_op: float32 [256, 128, 128], P(('mesh', 'src')), may hold values from -1 to 4
Outputs:
- correction: float32 [512, 24576], P('src', 'mesh')
The draws below stay inside these ranges and needn't reach their ends.
Inputs may be any that keep to these rules, and one draw needn't show every extreme that they name: `tail_node`: every value occurs. An edge of block k has head_node of (2 - k) * 128 or more; head_node never equals 256 + tail_node.
All inputs are finite; a program needn't handle non-finite values. No bound on the sum of `interior` on one device may be relied on, other than what follows from the above.
Results may differ from the reference program's by a relative error of at most 0.0034.
Values may be sent and summed in bfloat16 or wider, within the bound.
No kernel may reach another device: no remote copies, remote signals or barrier semaphores. Data moves between devices by JAX's collectives and lax.ppermute only.
A program may use at most 64 MiB of HBM per device.

```python
import math
import jax
import jax.numpy as jnp
from jax import lax

BLOCK_NODES = 128
TILES_BLOCK = 3
SOURCES = 512
EDGES = 24576
BLOCKS = 64
NODES = 8192


def incidence(key):
    tail_key = jax.random.fold_in(key, 11)
    head_key = jax.random.fold_in(key, 12)
    edge_span = TILES_BLOCK * BLOCK_NODES
    tail_pick = jax.random.randint(tail_key, (EDGES,), 0, BLOCK_NODES).astype(jnp.int32)
    edge_block = jnp.arange(EDGES, dtype=jnp.int32) // edge_span
    low_bound = (jnp.maximum(2 - edge_block, 0) * BLOCK_NODES).astype(jnp.int32)
    head_range = 3 * BLOCK_NODES - low_bound
    raw_pick = jax.random.randint(head_key, (EDGES,), 0, 3 * BLOCK_NODES).astype(jnp.int32)
    head_pick = low_bound + raw_pick % head_range
    clashing = head_pick == tail_pick + 2 * BLOCK_NODES
    head_pick = jnp.where(clashing, low_bound + (head_pick - low_bound + 1) % head_range, head_pick)
    return (tail_pick, head_pick.astype(jnp.int32))


def draw_tail_node(key, part):
    return incidence(key)[0]


def draw_head_node(key, part):
    return incidence(key)[1]


def block_matrix(key, low_diag, high_diag, off_scale):
    mat_shape = (4 * BLOCKS, BLOCK_NODES, BLOCK_NODES)
    diag_part = jnp.exp(jax.random.uniform(jax.random.fold_in(key, 21), mat_shape[:2], jnp.float32, math.log(low_diag), math.log(high_diag)))
    off_part = off_scale * jnp.clip(jax.random.normal(jax.random.fold_in(key, 22), mat_shape, jnp.float32), -5.0, 5.0)
    identity = jnp.eye(BLOCK_NODES, dtype=jnp.float32)
    return off_part * (1.0 - identity) + diag_part[:, :, None] * identity


def draw_block_op(key, part):
    return block_matrix(key, 2.0, 4.0, 0.08)


def draw_block_inv(key, part):
    return block_matrix(key, 0.25, 0.5, 0.01)


def touch_ends(values, key, least, largest):
    longest = values.shape.index(max(values.shape))
    spots = []
    for shift in (0, 1):
        where = [jax.random.randint(jax.random.fold_in(key, axis), (), 0, length) for axis, length in enumerate(values.shape)]
        where[longest] = (where[longest] + shift) % values.shape[longest]
        spots.append(tuple(where))
    return values.at[spots[0]].set(least).at[spots[1]].set(largest)


def shard_levels(key, shape, shards, smallest, top_value):
    def one(position, blocks):
        steps = jax.random.uniform(jax.random.fold_in(jax.random.fold_in(key, 6), position), (blocks,), jnp.float32, smallest / len(shards), top_value / len(shards))
        return jnp.repeat(jnp.exp(steps), shape[position] // blocks).reshape((-1,) + (1,) * (len(shape) - position - 1))

    gain = one(*shards[0])
    for cut in shards[1:]:
        gain = gain * one(*cut)
    return gain


def gaussian(rng, shape, width, bound, shards=(), held_as=jnp.bfloat16):
    result = width * jax.random.normal(rng, shape, jnp.float32)
    if shards:
        result = result * shard_levels(rng, shape, shards, -0.22, 0.18)
    return jnp.clip(result, -bound, bound).astype(held_as)


def setup_inputs(seed: int = 0) -> dict:
    keys = jax.random.split(jax.random.key(seed), 11)
    return {
        "solution": gaussian(keys[0], (SOURCES, EDGES), 1.0, 6.0, ((0, 4), (1, 8)), jnp.float32),
        "conduct": jnp.clip(jnp.exp(math.log(2.0) - 1.3862944 * jax.random.uniform(keys[1], (EDGES,), jnp.float32) ** shard_levels(keys[1], (EDGES,), ((0, 8),), -0.2, 0.2)), 0.5, 2.0),
        "source_edge": touch_ends(jax.random.randint(keys[2], (SOURCES,), 0, EDGES), jax.random.fold_in(keys[2], 1), 0, EDGES - 1).astype(jnp.int32),
        "source_amp": gaussian(keys[3], (SOURCES,), 2.0, 8.0, ((0, 4),), jnp.float32),
        "interior": touch_ends((jax.random.randint(keys[4], (NODES,), 0, 8) < 7).astype(jnp.int32), jax.random.fold_in(keys[4], 1), 0, 1),
        "edge_dir": gaussian(keys[5], (3, EDGES), 1.0, 4.0, ((1, 8),), jnp.float32),
        "tail_node": draw_tail_node(jax.random.fold_in(keys[10], 71), 0),
        "head_node": draw_head_node(jax.random.fold_in(keys[10], 71), 0),
        "block_inv": draw_block_inv(jax.random.fold_in(keys[10], 71), 0),
        "block_op": draw_block_op(jax.random.fold_in(keys[10], 71), 0),
    }


HIGHEST_PREC = lax.Precision.HIGHEST


def reference(solution, conduct, source_edge, source_amp, interior, edge_dir, tail_node, head_node, block_inv, block_op):
    source_count, edge_count = solution.shape
    edge_span = TILES_BLOCK * BLOCK_NODES
    edge_block = jnp.arange(edge_count, dtype=jnp.int32) // edge_span
    tail_glob = (edge_block * BLOCK_NODES + tail_node).astype(jnp.int32)
    head_glob = ((edge_block - 2) * BLOCK_NODES + head_node).astype(jnp.int32)
    residual = -conduct[None, :] * solution
    residual = residual.at[jnp.arange(source_count, dtype=jnp.int32), source_edge].add(source_amp)
    unit_row = jnp.ones((1, edge_count), jnp.float32)
    half_dir = 0.5 * edge_dir
    coef_tail = jnp.concatenate([-unit_row, half_dir], 0)
    coef_head = jnp.concatenate([unit_row, half_dir], 0)
    keep_mask = interior.astype(jnp.float32)[:, None]
    nblocks = NODES // BLOCK_NODES
    mats_inv = block_inv.reshape(nblocks, 4, BLOCK_NODES, BLOCK_NODES)
    mats_op = block_op.reshape(nblocks, 4, BLOCK_NODES, BLOCK_NODES)
    resid_t = residual.T
    output = jnp.zeros((edge_count, source_count), jnp.float32)
    for component in range(4):
        nodal_sum = jax.ops.segment_sum(coef_tail[component][:, None] * resid_t, tail_glob, NODES)
        nodal_sum = nodal_sum + jax.ops.segment_sum(coef_head[component][:, None] * resid_t, head_glob, NODES)
        rounded = lax.optimization_barrier((nodal_sum * keep_mask).astype(jnp.bfloat16))
        nodal_rhs = rounded.astype(jnp.float32).reshape(nblocks, BLOCK_NODES, source_count)
        inverse = mats_inv[:, component]
        operator = mats_op[:, component]
        first_pass = jnp.einsum('bnm,bms->bns', inverse, nodal_rhs, precision=HIGHEST_PREC)
        defect = nodal_rhs - jnp.einsum('bnm,bms->bns', operator, first_pass, precision=HIGHEST_PREC)
        solved = first_pass + jnp.einsum('bnm,bms->bns', inverse, defect, precision=HIGHEST_PREC)
        solved = lax.optimization_barrier(solved.reshape(NODES, source_count).astype(jnp.bfloat16))
        nodal = solved.astype(jnp.float32) * keep_mask
        output = output + coef_tail[component][:, None] * nodal[tail_glob] + coef_head[component][:, None] * nodal[head_glob]
    return output.T
```

```python
import jax
import jax.numpy as jnp
from jax import lax
from jax.experimental import pallas as pl
from jax.experimental.pallas import tpu as pltpu
from jax.sharding import PartitionSpec as P

BLOCK_NODES = 128
TILES_BLOCK = 3
SPAN = TILES_BLOCK * BLOCK_NODES
F32 = jnp.float32
BF16 = jnp.bfloat16


def split(x):
    high = x.astype(BF16)
    return high, (x - high.astype(F32)).astype(BF16)


def matmul3(a, b):
    a_hi, a_lo = split(a)
    b_hi, b_lo = split(b)
    left = jnp.concatenate([a_hi, a_hi, a_lo], 1)
    right = jnp.concatenate([b_hi, b_lo, b_hi], 0)
    return jnp.dot(left, right, preferred_element_type=F32)


def dot_nt(a, b):
    return lax.dot_general(a, b, (((1,), (1,)), ((), ())), preferred_element_type=F32)


def combine_kernel(inv_ref, op_ref, out_ref):
    pairs, n, _ = inv_ref.shape
    row = lax.broadcasted_iota(jnp.int32, (n, n), 0)
    on_diag = row == lax.broadcasted_iota(jnp.int32, (n, n), 1)
    rests = []
    for i in range(pairs):
        inverse = inv_ref[i]
        full = 2.0 * inverse - matmul3(inverse, matmul3(op_ref[i], inverse))
        rounded = full.astype(BF16)
        out_ref[i * n : (i + 1) * n, :] = rounded
        rest = jnp.where(on_diag, full - rounded.astype(F32), 0.0)
        rests.append(jnp.sum(rest, axis=0, keepdims=True))
    pad = out_ref.shape[0] - pairs * n - pairs
    rests.append(jnp.zeros((pad, n), F32))
    out_ref[pairs * n :, :] = jnp.concatenate(rests, 0).astype(BF16)


def combine(inv, op):
    pairs, n, _ = inv.shape
    rows = pairs * n + (pairs + 15) // 16 * 16
    return pl.pallas_call(
        combine_kernel, out_shape=jax.ShapeDtypeStruct((rows, n), BF16), name="combine"
    )(inv, op)


def incidence(tail, head):
    n = BLOCK_NODES
    early = lax.broadcasted_iota(jnp.int32, (2 * n, SPAN), 0) == head
    at_node = lax.broadcasted_iota(jnp.int32, (n, SPAN), 0)
    is_head = at_node + 2 * n == head
    is_tail = at_node == tail
    one = lambda m, v: jnp.where(m, 1.0, v)
    early = one(early, 0.0).astype(BF16)
    plus = one(is_head, one(is_tail, 0.0)).astype(BF16)
    minus = one(is_head, jnp.where(is_tail, -1.0, 0.0)).astype(BF16)
    return early, plus, minus


def restrict_kernel(first, count, carried, *refs):
    (start_ref, sol_ref, cond_ref, edge_ref, amp_ref, dir_ref, tail_ref, head_ref, keep_ref) = refs[:9]
    refs = refs[9:]
    if carried:
        carry_in, out_ref, carry_out, acc, edge_col, amp_col = refs
    else:
        out_ref, carry_out, acc, edge_col, amp_col = refs
    n = BLOCK_NODES
    sources = sol_ref.shape[0]
    step = pl.program_id(0)
    k = step + first

    @pl.when(step == 0)
    def _():
        acc[...] = carry_in[...] if carried else jnp.zeros_like(acc)
        edge_col[...] = jnp.broadcast_to(edge_ref[...], (n, sources)).T
        amp_col[...] = jnp.broadcast_to(amp_ref[...], (n, sources)).T

    here = pl.ds(pl.multiple_of(k * SPAN, n), SPAN)
    lane = lax.broadcasted_iota(jnp.int32, (sources, SPAN), 1) + (start_ref[0] + k * SPAN)
    hit = jnp.concatenate([edge_col[...]] * TILES_BLOCK, 1) == lane
    amp = jnp.concatenate([amp_col[...]] * TILES_BLOCK, 1)
    residual = jnp.where(hit, amp, 0.0) - cond_ref[:, here] * sol_ref[...]
    half = 0.5 * dir_ref[:, here]
    values = [residual] + [residual * half[c : c + 1] for c in range(3)]
    early, plus, minus = incidence(tail_ref[:, here], head_ref[:, here])
    high, low = split(jnp.concatenate(values, 0))
    near = dot_nt(high, early) + dot_nt(low, early)
    grad = dot_nt(high[:sources], minus) + dot_nt(low[:sources], minus)
    vect = dot_nt(high[sources:], plus) + dot_nt(low[sources:], plus)
    done = acc[:, :n] + near[:, :n]
    acc[:, :n] = acc[:, n:] + near[:, n:]
    acc[:, n:] = jnp.concatenate([grad, vect], 0)
    if carried:
        keep = keep_ref[:, pl.ds(pl.multiple_of((k - 2) * n, n), n)]
        done = done * keep.astype(F32)
    out_ref[0] = done.astype(out_ref.dtype)

    @pl.when(step == count - 1)
    def _():
        carry_out[...] = acc[...]


def restrict(first, count, args, carry):
    start, sol = args[:2]
    n = BLOCK_NODES
    sources = sol.shape[0]
    whole = lambda x: pl.BlockSpec(x.shape, lambda i, *_: (0,) * x.ndim)
    carried = carry is not None
    ins = args[1:] + ((carry,) if carried else ())
    specs = [pl.BlockSpec((sources, SPAN), lambda i, *_: (0, i + first))]
    specs += [whole(x) for x in ins[1:]]
    shapes = (
        jax.ShapeDtypeStruct((count, 4 * sources, n), BF16 if carried else F32),
        jax.ShapeDtypeStruct((4 * sources, 2 * n), F32),
    )
    return pl.pallas_call(
        lambda *refs: restrict_kernel(first, count, carried, *refs),
        out_shape=shapes,
        grid_spec=pltpu.PrefetchScalarGridSpec(
            num_scalar_prefetch=1,
            grid=(count,),
            in_specs=specs,
            out_specs=(
                pl.BlockSpec((1, 4 * sources, n), lambda i, *_: (i, 0, 0)),
                pl.BlockSpec((4 * sources, 2 * n), lambda i, *_: (0, 0)),
            ),
            scratch_shapes=[
                pltpu.VMEM((4 * sources, 2 * n), F32),
                pltpu.VMEM((sources, n), jnp.int32),
                pltpu.VMEM((sources, n), F32),
            ],
        ),
        name="restrict_rest" if carried else "restrict_rim",
    )(start, *ins)


def sweep(values, mats_ref, i, per_owner, keep):
    n = BLOCK_NODES
    sources = values.shape[0] // 4
    pairs = 4 * per_owner
    solved = []
    for c in range(4):
        j = 4 * i + c
        part = values[c * sources : (c + 1) * sources]
        rest = mats_ref[pairs * n + j : pairs * n + j + 1, :].astype(F32)
        matrix = mats_ref[j * n : (j + 1) * n, :]
        solved.append(dot_nt(part, matrix) + part.astype(F32) * rest)
    return (jnp.concatenate(solved, 0).astype(BF16).astype(F32) * keep).astype(BF16)


def last_kernel(nblocks, owners, *refs):
    place_ref = refs[0]
    mats = refs[1 : 1 + owners]
    carry_ref, rim_ref, keep_ref, out_ref = refs[1 + owners :]
    n = BLOCK_NODES
    per_owner = nblocks // owners
    for d in range(owners):
        for i in range(per_owner):
            block = (place_ref[0] ^ d) * per_owner + i

            @pl.when(block >= nblocks - 2)
            def _():
                at = block - (nblocks - 2)
                keep = keep_ref[:, pl.ds(pl.multiple_of(block * n, n), n)].astype(F32)
                total = carry_ref[:, pl.ds(pl.multiple_of(at * n, n), n)] + rim_ref[at]
                values = (total * keep).astype(BF16)
                out_ref[at] = sweep(values, mats[d], i, per_owner, keep)


def last_blocks(nblocks, place, mats, carry, rim, keep):
    return pl.pallas_call(
        lambda *refs: last_kernel(nblocks, len(mats), *refs),
        out_shape=jax.ShapeDtypeStruct(rim.shape, BF16),
        grid_spec=pltpu.PrefetchScalarGridSpec(num_scalar_prefetch=1, grid=()),
        name="sweep_last",
    )(place, *mats, carry, rim, keep)


def prolong(window, tail, head, directions, sources):
    early, plus, minus = incidence(tail, head)
    n = BLOCK_NODES
    old = jnp.concatenate([window[0], window[1]], 1)
    near = jnp.dot(old, early, preferred_element_type=F32)
    grad = jnp.dot(window[2][:sources], minus, preferred_element_type=F32)
    vect = jnp.dot(window[2][sources:], plus, preferred_element_type=F32)
    half = 0.5 * directions
    total = near[:sources] + grad
    for c in range(3):
        part = near[(c + 1) * sources : (c + 2) * sources] + vect[c * sources : (c + 1) * sources]
        total = total + half[c : c + 1] * part
    return total


def rest_kernel(nblocks, owners, *refs):
    place_ref = refs[0]
    mats = refs[1 : 1 + owners]
    (val_ref, last_ref, keep_ref, dir_ref, tail_ref, head_ref, out_ref, front_ref, nodal) = refs[1 + owners :]
    n = BLOCK_NODES
    per_owner = nblocks // owners
    sources = out_ref.shape[0]
    step = pl.program_id(0)

    @pl.when(step == 0)
    def _():
        nodal[nblocks - 2 :] = last_ref[...]
        for d in range(owners):
            for i in range(per_owner):
                block = (place_ref[0] ^ d) * per_owner + i

                @pl.when(block < nblocks - 2)
                def _():
                    keep = keep_ref[:, pl.ds(pl.multiple_of(block * n, n), n)].astype(F32)
                    nodal[block] = sweep(val_ref[block], mats[d], i, per_owner, keep)

        front_ref[...] = nodal[:2]

    here = pl.ds(pl.multiple_of((step + 2) * SPAN, n), SPAN)
    window = [nodal[step], nodal[step + 1], nodal[step + 2]]
    out_ref[...] = prolong(window, tail_ref[:, here], head_ref[:, here], dir_ref[:, here], sources)


def rest_blocks(nblocks, place, mats, values, last, keep, directions, tail, head):
    n = BLOCK_NODES
    sources = values.shape[1] // 4
    ins = tuple(mats) + (values, last, keep, directions, tail, head)
    whole = lambda x: pl.BlockSpec(x.shape, lambda i, *_: (0,) * x.ndim)
    return pl.pallas_call(
        lambda *refs: rest_kernel(nblocks, len(mats), *refs),
        out_shape=(
            jax.ShapeDtypeStruct((sources, nblocks * SPAN), F32),
            jax.ShapeDtypeStruct((2, 4 * sources, n), BF16),
        ),
        grid_spec=pltpu.PrefetchScalarGridSpec(
            num_scalar_prefetch=1,
            grid=(nblocks - 2,),
            in_specs=[whole(x) for x in ins],
            out_specs=(
                pl.BlockSpec((sources, SPAN), lambda i, *_: (0, i + 2)),
                pl.BlockSpec((2, 4 * sources, n), lambda i, *_: (0, 0, 0)),
            ),
            scratch_shapes=[pltpu.VMEM((nblocks, 4 * sources, n), BF16)],
        ),
        name="sweep_prolong",
    )(place, *ins)


def front_kernel(earlier_ref, front_ref, dir_ref, tail_ref, head_ref, old_ref, out_ref, nodal):
    n = BLOCK_NODES
    step = pl.program_id(0)
    nodal[:2] = earlier_ref[...]
    nodal[2:] = front_ref[...]
    here = pl.ds(pl.multiple_of(step * SPAN, n), SPAN)
    window = [nodal[step], nodal[step + 1], nodal[step + 2]]
    out_ref[...] = prolong(
        window, tail_ref[:, here], head_ref[:, here], dir_ref[:, here], out_ref.shape[0]
    )


def front_blocks(earlier, front, directions, tail, head, out):
    n = BLOCK_NODES
    sources = out.shape[0]
    ins = (earlier, front, directions, tail, head)
    specs = [pl.BlockSpec(x.shape, lambda i, x=x: (0,) * x.ndim) for x in ins]
    return pl.pallas_call(
        front_kernel,
        out_shape=jax.ShapeDtypeStruct(out.shape, out.dtype),
        grid=(2,),
        in_specs=specs + [pl.BlockSpec(memory_space=pl.ANY)],
        out_specs=pl.BlockSpec((sources, SPAN), lambda i: (0, i)),
        scratch_shapes=[pltpu.VMEM((4, 4 * sources, n), BF16)],
        input_output_aliases={len(ins): 0},
        name="prolong_front",
    )(*ins, out)


def shifted(x, axis, by):
    peers = lax.axis_size(axis)
    pairs = [(i, i + by) for i in range(peers) if 0 <= i + by < peers]
    return lax.ppermute(x, axis, pairs)


def exchange(x, axis, d):
    return lax.ppermute(x, axis, [(i, i ^ d) for i in range(lax.axis_size(axis))])


def shards(
    solution,
    conduct,
    source_edge,
    source_amp,
    interior,
    edge_dir,
    tail_node,
    head_node,
    block_inv,
    block_op,
):
    edge_dev = solution.shape[1]
    nblocks = edge_dev // SPAN
    owners = lax.axis_size("src")
    first_edge = (lax.axis_index("mesh") * edge_dev).astype(jnp.int32).reshape(1)
    place = lax.axis_index("src").astype(jnp.int32).reshape(1)
    row = lambda x: x.reshape(1, -1)
    tail, head, keep = row(tail_node), row(head_node), row(interior)

    own = combine(block_inv, block_op)
    far = {d: exchange(own, "src", d) for d in range(owners - 1, 0, -1)}
    mats = [own] + [far[d] for d in range(1, owners)]

    args = (first_edge, solution, row(conduct), row(source_edge), row(source_amp), edge_dir, tail, head, keep)
    rim, carry = restrict(0, 2, args, None)
    rim = shifted(rim, "mesh", -1)
    values, carry = restrict(2, nblocks - 2, args, carry)

    last = last_blocks(nblocks, place, mats, carry, rim, keep)
    earlier = shifted(last, "mesh", 1)
    out, front = rest_blocks(nblocks, place, mats, values, last, keep, edge_dir, tail, head)
    return front_blocks(earlier, front, edge_dir, tail, head, out)


def solution(mesh):
    placed = (
        P("src", "mesh"),
        P("mesh"),
        P("src"),
        P("src"),
        P("mesh"),
        P(None, "mesh"),
        P("mesh"),
        P("mesh"),
        P(("mesh", "src"), None, None),
        P(("mesh", "src"), None, None),
    )
    return jax.shard_map(
        shards, mesh=mesh, in_specs=placed, out_specs=P("src", "mesh"), check_vma=False
    )
```

```python
import jax
import jax.numpy as jnp
from jax import lax
from jax.experimental import pallas as pl
from jax.experimental.pallas import tpu as pltpu
from jax.sharding import PartitionSpec as P

BLOCK_NODES = 128
TILES_BLOCK = 3
SPAN = TILES_BLOCK * BLOCK_NODES
F32 = jnp.float32
BF16 = jnp.bfloat16


PARAMS = pltpu.CompilerParams(vmem_limit_bytes=24 << 20)


def local(x):
    return pltpu.with_memory_space_constraint(x, pltpu.VMEM)


def held(x):
    return pl.BlockSpec(memory_space=pltpu.VMEM)


def split(x):
    high = x.astype(BF16)
    return high, (x - high.astype(F32)).astype(BF16)


def matmul3(a, b):
    (a_hi, a_lo), (b_hi, b_lo) = a, b
    left = jnp.concatenate([a_hi, a_hi, a_lo], 1)
    right = jnp.concatenate([b_hi, b_lo, b_hi], 0)
    return jnp.dot(left, right, preferred_element_type=F32)


def dot_nt(a, b):
    return lax.dot_general(a, b, (((1,), (1,)), ((), ())), preferred_element_type=F32)


def half_rows(half):
    return half * BLOCK_NODES + (half + 15) // 16 * 16


def combine_kernel(inv_ref, op_ref, *refs):
    sems = refs[-1]
    count = (len(refs) - 2) // 2
    out_ref = refs[count]
    fetched = refs[count + 1 : -1]
    half, n, _ = inv_ref.shape
    at = pl.program_id(0)
    copies = [pltpu.make_async_copy(refs[i], fetched[i], sems.at[i]) for i in range(count)]

    @pl.when(at == 0)
    def _():
        for copy in copies:
            copy.start()

    row = lax.broadcasted_iota(jnp.int32, (n, n), 0)
    on_diag = row == lax.broadcasted_iota(jnp.int32, (n, n), 1)
    rests = []
    for i in range(half):
        inverse = inv_ref[i]
        parts = split(inverse)
        full = 2.0 * inverse - matmul3(parts, split(matmul3(split(op_ref[i]), parts)))
        rounded = full.astype(BF16)
        out_ref[at, i * n : (i + 1) * n, :] = rounded
        rest = jnp.where(on_diag, full - rounded.astype(F32), 0.0)
        rests.append(jnp.sum(rest, axis=0, keepdims=True))
    pad = out_ref.shape[1] - half * n - half
    rests.append(jnp.zeros((pad, n), F32))
    out_ref[at, half * n :, :] = jnp.concatenate(rests, 0).astype(BF16)

    @pl.when(at == pl.num_programs(0) - 1)
    def _():
        for copy in copies:
            copy.wait()


def combine(inv, op, *others):
    pairs, n, _ = inv.shape
    half = pairs // 2
    spec = pl.BlockSpec((half, n, n), lambda i: (i, 0, 0))
    far = lambda x: pltpu.with_memory_space_constraint(x, pltpu.HBM)
    return pl.pallas_call(
        combine_kernel,
        out_shape=(
            pltpu.VMEM((2, half_rows(half), n), BF16),
            *(pltpu.VMEM(x.shape, x.dtype) for x in others),
        ),
        grid=(2,),
        in_specs=[spec, spec] + [pl.BlockSpec(memory_space=pltpu.HBM) for x in others],
        out_specs=(held(None),) * (1 + len(others)),
        scratch_shapes=[pltpu.SemaphoreType.DMA((len(others),))],
        compiler_params=PARAMS,
        name="combine",
    )(*(far(x) for x in (inv, op, *others)))


def incidence(tail, head):
    n = BLOCK_NODES
    early = lax.broadcasted_iota(jnp.int32, (2 * n, SPAN), 0) == head
    at_node = lax.broadcasted_iota(jnp.int32, (n, SPAN), 0)
    is_head = at_node + 2 * n == head
    is_tail = at_node == tail
    one = lambda m, v: jnp.where(m, 1.0, v)
    early = one(early, 0.0).astype(BF16)
    plus = one(is_head, one(is_tail, 0.0)).astype(BF16)
    minus = one(is_head, jnp.where(is_tail, -1.0, 0.0)).astype(BF16)
    return early, plus, minus


def restrict_kernel(first, carried, *refs):
    start_ref, sol_ref, cond_ref, edge_ref, amp_ref, dir_ref, tail_ref, head_ref, keep_ref = refs[:9]
    carry_ref = refs[9] if carried else None
    out_ref, acc, edge_col, amp_col = refs[-4:]
    n = BLOCK_NODES
    sources = sol_ref.shape[0]
    step = pl.program_id(0)
    k = step + first

    @pl.when(step == 0)
    def _():
        acc[...] = carry_ref[...] if carried else jnp.zeros_like(acc)
        edge_col[...] = jnp.broadcast_to(edge_ref[...], (n, sources)).T
        amp_col[...] = jnp.broadcast_to(amp_ref[...], (n, sources)).T

    here = pl.ds(pl.multiple_of(k * SPAN, n), SPAN)
    lane = lax.broadcasted_iota(jnp.int32, (sources, SPAN), 1) + (start_ref[0] + k * SPAN)
    hit = jnp.concatenate([edge_col[...]] * TILES_BLOCK, 1) == lane
    amp = jnp.concatenate([amp_col[...]] * TILES_BLOCK, 1)
    residual = jnp.where(hit, amp, 0.0) - cond_ref[:, here] * sol_ref[:, here]
    half = 0.5 * dir_ref[:, here]
    values = [residual] + [residual * half[c : c + 1] for c in range(3)]
    early, plus, minus = incidence(tail_ref[:, here], head_ref[:, here])
    high, low = split(jnp.concatenate(values, 0))
    near = dot_nt(high, early) + dot_nt(low, early)
    grad = dot_nt(high[:sources], minus) + dot_nt(low[:sources], minus)
    vect = dot_nt(high[sources:], plus) + dot_nt(low[sources:], plus)
    done = acc[:, :n] + near[:, :n]
    acc[:, :n] = acc[:, n:] + near[:, n:]
    acc[:, n:] = jnp.concatenate([grad, vect], 0)
    if carried:
        keep = keep_ref[:, pl.ds(pl.multiple_of((k - 2) * n, n), n)]
        done = done * keep.astype(F32)
    out_ref[step] = done.astype(out_ref.dtype)


def restrict(first, count, start, ins, carry):
    n = BLOCK_NODES
    sources = ins[0].shape[0]
    carried = carry is not None
    if carried:
        ins += (local(carry),)
    return pl.pallas_call(
        lambda *refs: restrict_kernel(first, carried, *refs),
        out_shape=(
            pltpu.VMEM((count, 4 * sources, n), BF16 if carried else F32),
            pltpu.VMEM((4 * sources, 2 * n), F32),
        ),
        grid_spec=pltpu.PrefetchScalarGridSpec(
            num_scalar_prefetch=1,
            grid=(count,),
            in_specs=[held(x) for x in ins],
            out_specs=(held(None), held(None)),
            scratch_shapes=[
                pltpu.VMEM((sources, n), jnp.int32),
                pltpu.VMEM((sources, n), F32),
            ],
        ),
        compiler_params=PARAMS,
        name="restrict_rest" if carried else "restrict_rim",
    )(start, *ins)


def unpack(refs, owners):
    own = refs[0]
    mats = [[own.at[0], own.at[1]]]
    refs = refs[1:]
    for d in range(1, owners):
        if len(refs[0].shape) == 3:
            mats.append([refs[0].at[0], refs[0].at[1]])
            refs = refs[1:]
        else:
            mats.append(list(refs[:2]))
            refs = refs[2:]
    return mats


def sweep(values, halves, i, half, keep):
    n = BLOCK_NODES
    sources = values.shape[0] // 4
    solved = []
    for c in range(4):
        h, j = divmod(4 * i + c, half)
        part = values[c * sources : (c + 1) * sources]
        rest = halves[h][half * n + j : half * n + j + 1, :].astype(F32)
        matrix = halves[h][j * n : (j + 1) * n, :]
        solved.append((dot_nt(part, matrix) + part.astype(F32) * rest) * keep)
    return jnp.concatenate(solved, 0).astype(BF16)


def each_block(place_ref, mats, per_owner, keep_ref, todo):
    n = BLOCK_NODES
    for d, halves in enumerate(mats):
        for i in range(per_owner):
            block = (place_ref[0] ^ d) * per_owner + i
            keep = keep_ref[:, pl.ds(pl.multiple_of(block * n, n), n)].astype(F32)
            todo(block, lambda values: sweep(values, halves, i, 2 * per_owner, keep), keep)


def last_kernel(nblocks, owners, place_ref, *refs):
    carry_ref, rim_ref, keep_ref, out_ref = refs[-4:]
    n = BLOCK_NODES
    per_owner = nblocks // owners

    def todo(block, solve, keep):
        @pl.when(block >= nblocks - 2)
        def _():
            at = block - (nblocks - 2)
            total = carry_ref[:, pl.ds(pl.multiple_of(at * n, n), n)] + rim_ref[at]
            out_ref[at] = solve((total * keep).astype(BF16))

    each_block(place_ref, unpack(refs[:-4], owners), per_owner, keep_ref, todo)


def last_blocks(nblocks, owners, place, mats, carry, rim, keep):
    ins = [local(x) for x in (*mats, carry, rim, keep)]
    return pl.pallas_call(
        lambda *refs: last_kernel(nblocks, owners, *refs),
        out_shape=pltpu.VMEM(rim.shape, BF16),
        grid_spec=pltpu.PrefetchScalarGridSpec(
            num_scalar_prefetch=1,
            grid=(),
            in_specs=[held(x) for x in ins],
            out_specs=held(None),
        ),
        compiler_params=PARAMS,
        name="sweep_last",
    )(place, *ins)


def prolong(window, tail, head, directions, sources):
    early, plus, minus = incidence(tail, head)
    old = jnp.concatenate([window[0], window[1]], 1)
    near = jnp.dot(old, early, preferred_element_type=F32)
    grad = jnp.dot(window[2][:sources], minus, preferred_element_type=F32)
    vect = jnp.dot(window[2][sources:], plus, preferred_element_type=F32)
    half = 0.5 * directions
    total = near[:sources] + grad
    for c in range(3):
        part = near[(c + 1) * sources : (c + 2) * sources] + vect[c * sources : (c + 1) * sources]
        total = total + half[c : c + 1] * part
    return total


def rest_kernel(nblocks, owners, parts, place_ref, *refs):
    last_ref, keep_ref, dir_ref, tail_ref, head_ref, out_ref, front_ref, nodal = refs[-8:]
    value_refs = refs[-8 - len(parts) : -8]
    per_owner = nblocks // owners
    sources = out_ref.shape[0]
    step = pl.program_id(0)

    @pl.when(step == 0)
    def _():
        at = 0
        for ref, count in zip(value_refs, parts):
            nodal[at : at + count] = ref[...]
            at += count
        nodal[nblocks - 2 :] = last_ref[...]

        def todo(block, solve, keep):
            @pl.when(block < nblocks - 2)
            def _():
                nodal[block] = solve(nodal[block])

        mats = unpack(refs[: -8 - len(parts)], owners)
        each_block(place_ref, mats, per_owner, keep_ref, todo)
        front_ref[...] = nodal[:2]

    here = pl.ds(pl.multiple_of((step + 2) * SPAN, BLOCK_NODES), SPAN)
    window = [nodal[step], nodal[step + 1], nodal[step + 2]]
    out_ref[...] = prolong(window, tail_ref[:, here], head_ref[:, here], dir_ref[:, here], sources)


def rest_blocks(nblocks, owners, place, mats, values, last, keep, directions, tail, head):
    n = BLOCK_NODES
    sources = last.shape[1] // 4
    parts = [x.shape[0] for x in values]
    ins = [local(x) for x in (*mats, *values, last, keep, directions, tail, head)]
    return pl.pallas_call(
        lambda *refs: rest_kernel(nblocks, owners, parts, *refs),
        out_shape=(
            jax.ShapeDtypeStruct((sources, nblocks * SPAN), F32),
            pltpu.VMEM(last.shape, BF16),
        ),
        grid_spec=pltpu.PrefetchScalarGridSpec(
            num_scalar_prefetch=1,
            grid=(nblocks - 2,),
            in_specs=[held(x) for x in ins],
            out_specs=(pl.BlockSpec((sources, SPAN), lambda i, *_: (0, i + 2)), held(None)),
            scratch_shapes=[pltpu.VMEM((nblocks, 4 * sources, n), BF16)],
        ),
        compiler_params=PARAMS,
        name="sweep_prolong",
    )(place, *ins)


def front_kernel(earlier_ref, front_ref, dir_ref, tail_ref, head_ref, old_ref, out_ref):
    n = BLOCK_NODES
    sources = out_ref.shape[0]
    nodal = [earlier_ref[0], earlier_ref[1], front_ref[0], front_ref[1]]
    for k in range(2):
        here = slice(k * SPAN, (k + 1) * SPAN)
        out_ref[:, here] = prolong(
            nodal[k : k + 3], tail_ref[:, here], head_ref[:, here], dir_ref[:, here], sources
        )


def front_blocks(earlier, front, directions, tail, head, out):
    sources = out.shape[0]
    ins = [local(x) for x in (earlier, front, directions, tail, head)]
    return pl.pallas_call(
        front_kernel,
        out_shape=jax.ShapeDtypeStruct(out.shape, out.dtype),
        grid=(1,),
        in_specs=[held(x) for x in ins] + [pl.BlockSpec(memory_space=pl.ANY)],
        out_specs=pl.BlockSpec((sources, 2 * SPAN), lambda i: (0, 0)),
        input_output_aliases={len(ins): 0},
        compiler_params=PARAMS,
        name="prolong_front",
    )(*ins, out)


def shifted(x, axis, by):
    peers = lax.axis_size(axis)
    pairs = [(i, i + by) for i in range(peers) if 0 <= i + by < peers]
    return lax.ppermute(x, axis, pairs)


def exchange(x, axis, d):
    return lax.ppermute(x, axis, [(i, i ^ d) for i in range(lax.axis_size(axis))])


def after(x, *earlier):
    return lax.optimization_barrier((x, *earlier))[0]


def shards(
    solution,
    conduct,
    source_edge,
    source_amp,
    interior,
    edge_dir,
    tail_node,
    head_node,
    block_inv,
    block_op,
):
    edge_dev = solution.shape[1]
    nblocks = edge_dev // SPAN
    owners = lax.axis_size("src")
    first_edge = (lax.axis_index("mesh") * edge_dev).astype(jnp.int32).reshape(1)
    place = lax.axis_index("src").astype(jnp.int32).reshape(1)
    row = lambda x: x.reshape(1, -1)
    ins = [solution, row(conduct), row(source_edge), row(source_amp), edge_dir]
    ins += [row(tail_node), row(head_node), row(interior)]

    own, *ins = combine(block_inv, block_op, *ins)
    far = [exchange(own, "src", d) for d in range(1, owners if owners != 4 else 3)]
    ins = tuple(local(x) for x in ins)
    edge_dir, tail, head, keep = ins[4:]
    rim, carry = restrict(0, 2, first_edge, ins, None)
    rim = shifted(rim, "mesh", -1)
    some = (nblocks - 2) // 2
    early, carry = restrict(2, some, first_edge, ins, carry)
    if owners == 4:
        first_edge = after(first_edge, *far)
        far += [exchange(far[0][0], "src", 2), exchange(far[1][1], "src", 1)]
    late, carry = restrict(2 + some, nblocks - 2 - some, first_edge, ins, carry)

    mats = [own] + far
    last = last_blocks(nblocks, owners, place, mats, carry, rim, keep)
    earlier = shifted(last, "mesh", 1)
    out, front = rest_blocks(
        nblocks, owners, place, mats, (early, late), last, keep, edge_dir, tail, head
    )
    return front_blocks(earlier, front, edge_dir, tail, head, out)


def solution(mesh):
    placed = (
        P("src", "mesh"),
        P("mesh"),
        P("src"),
        P("src"),
        P("mesh"),
        P(None, "mesh"),
        P("mesh"),
        P("mesh"),
        P(("mesh", "src"), None, None),
        P(("mesh", "src"), None, None),
    )
    return jax.shard_map(
        shards, mesh=mesh, in_specs=placed, out_specs=P("src", "mesh"), check_vma=False
    )
```
